256 devices in a mesh: row: 4 (over x_hi, core), col: 8 (over z), layer: 8 (over x_lo, y).
Axes of the slice: x: 4 (x_hi: 2, x_lo: 2; x = x_hi * 2 + x_lo), y: 4, z: 8, core: 2. Of those that a mesh axis runs over, the one named last changes fastest.
Arguments:
- amplitudes: float32 [12288, 16384], P(('row', 'col', 'layer')), may hold values from -6 to 6
- integrals: float32 [16384, 2048], P(('col', 'layer')), may hold values from -0.046875 to 0.046875
- pair_list: int32 [12288, 2], P(('row', 'col', 'layer')), may hold values from 0 to 199, as said below
- occupied_energy: float32 [200], replicated, may hold values from -1.5 to -0.3
- virtual_energy: float32 [2048], replicated, may hold values from 1 to 4
Outputs:
- ladder_update: float32 [12288, 2048], P(('row', 'col', 'layer'))
The draws below stay inside these ranges and needn't reach their ends.
Inputs may be any that keep to these rules, and one draw needn't show every extreme that they name: `pair_list`: each row (i, j) holds two occupied orbital numbers with i <= j.
All inputs are finite; a program needn't handle non-finite values.
Results may differ from the reference program's by a relative error of at most 0.000071.
Values sent between devices are 32-bit elements; how exact they have to be, the bound alone decides.
No kernel may reach another device: no remote copies, remote signals or barrier semaphores. Data moves between devices by JAX's collectives and lax.ppermute only.
A program may use at most 128 MiB of HBM per device.

```python
import jax
import jax.numpy as jnp
from jax import lax

NOCC = 200
K_EF = 16384
N_AB = 2048
PAIRS = 12288


def draw_pair_list(key, part):
    own_key = jax.random.fold_in(key, 7)
    key_one, key_two = jax.random.split(own_key)
    draw_one = jax.random.randint(key_one, (PAIRS,), 0, NOCC, dtype=jnp.int32)
    draw_two = jax.random.randint(key_two, (PAIRS,), 0, NOCC, dtype=jnp.int32)
    lower = jnp.minimum(draw_one, draw_two)
    upper = jnp.maximum(draw_one, draw_two)
    row_index = jnp.arange(PAIRS, dtype=jnp.int32)
    lower = jnp.where(row_index == 0, 0, lower)
    upper = jnp.where(row_index == 0, NOCC - 1, upper)
    return jnp.stack([lower, upper], axis=1).astype(jnp.int32)


def shard_levels(key, extent, cuts, low, high):
    def one(dim, shards_of):
        draws = jax.random.uniform(jax.random.fold_in(jax.random.fold_in(key, 6), dim), (shards_of,), jnp.float32, low / len(cuts), high / len(cuts))
        return jnp.repeat(jnp.exp(draws), extent[dim] // shards_of).reshape((-1,) + (1,) * (len(extent) - dim - 1))

    gain = one(*cuts[0])
    for cut in cuts[1:]:
        gain = gain * one(*cut)
    return gain


def bell_draw(stream_key, shape, scale, bound, pieces=(), kind=jnp.bfloat16):
    gain = shard_levels(stream_key, shape, pieces, -0.22, 0.18) if pieces else 1.0
    values = jax.random.normal(stream_key, shape, jnp.float32) * scale * gain
    return jnp.minimum(jnp.maximum(values, -bound), bound).astype(kind)


def setup_inputs(seed: int = 0) -> dict:
    key_list = jax.random.split(jax.random.key(seed), 6)
    return {
        "amplitudes": bell_draw(key_list[0], (PAIRS, K_EF), 1.0, 6.0, ((0, 256),), jnp.float32),
        "integrals": bell_draw(key_list[1], (K_EF, N_AB), K_EF ** -0.5, 0.046875, ((0, 64),), jnp.float32),
        "pair_list": draw_pair_list(jax.random.fold_in(key_list[5], 71), 0),
        "occupied_energy": jnp.clip(jax.random.uniform(key_list[3], (NOCC,), jnp.float32, -1.5, -0.3), -1.5, -0.3),
        "virtual_energy": jnp.clip(jax.random.uniform(key_list[4], (N_AB,), jnp.float32, 1.0, 4.0), 1.0, 4.0),
    }


def reference(amplitudes, integrals, pair_list, occupied_energy, virtual_energy):
    ladder = jnp.dot(amplitudes, integrals, precision=lax.Precision.HIGHEST, preferred_element_type=jnp.float32)
    occ_first = occupied_energy[pair_list[:, 0]]
    occ_second = occupied_energy[pair_list[:, 1]]
    denominator = virtual_energy[None, :] - occ_first[:, None] - occ_second[:, None]
    return ladder / denominator
```

```python
import functools

import jax
import jax.numpy as jnp
from jax import lax
from jax.experimental import pallas as pl
from jax.experimental.pallas import tpu as pltpu
from jax.sharding import Mesh
from jax.sharding import PartitionSpec as P


AXES = ("xhi", "core", "z", "xlo", "y")
LAYERS = 8
RING = 8
CHAINS = (256, 256, 256, 256)
GROUPS = ((0, 1), (2, 3))


def energy_lookup(pair_list, occupied_energy):
    occ_index = jnp.arange(occupied_energy.shape[0], dtype=jnp.int32)
    occ_first = jnp.sum(
        jnp.where(pair_list[:, 0:1] == occ_index[None, :], occupied_energy[None, :], 0.0), axis=1
    )
    occ_second = jnp.sum(
        jnp.where(pair_list[:, 1:2] == occ_index[None, :], occupied_energy[None, :], 0.0), axis=1
    )
    return (occ_first, occ_second)


def shift(value, axis, step):
    count = lax.axis_size(axis)
    return lax.ppermute(value, axis, [(i, (i + step) % count) for i in range(count)])


def roll_kernel(z_ref, amp_ref, out_ref):
    depth = out_ref.shape[2]
    for layer in range(LAYERS):
        out_ref[layer] = amp_ref[:, layer * depth : (layer + 1) * depth]


def roll_amplitudes(amplitudes, z, depth):
    rows = amplitudes.shape[0]
    return pl.pallas_call(
        roll_kernel,
        grid_spec=pltpu.PrefetchScalarGridSpec(
            num_scalar_prefetch=1,
            grid=(RING,),
            in_specs=[
                pl.BlockSpec((rows, LAYERS * depth), lambda s, z_ref: (0, lax.rem(z_ref[0] + s, RING)))
            ],
            out_specs=pl.BlockSpec((LAYERS, rows, depth), lambda s, z_ref: (0, 0, s)),
        ),
        out_shape=jax.ShapeDtypeStruct((LAYERS, rows, RING * depth), jnp.float32),
        cost_estimate=pl.CostEstimate(flops=0, bytes_accessed=8 * amplitudes.size, transcendentals=0),
        name="roll",
    )(z, amplitudes)


def split(value):
    high = value.astype(jnp.bfloat16)
    low = (value - high.astype(jnp.float32)).astype(jnp.bfloat16)
    return high, low


def product_kernel(places, core_ref, own_ref, other_ref, *refs):
    blocks, out_ref, high_ref, low_ref = refs[:-3], refs[-3], refs[-2], refs[-1]
    rows = own_ref.shape[0]
    for (offset, column), block in zip(places, blocks):
        high, low = split(block[...])
        depth, width = block.shape
        high_ref[offset : offset + depth, column : column + width] = high
        low_ref[offset : offset + depth, column : column + width] = low
    dot = functools.partial(jnp.dot, preferred_element_type=jnp.float32)
    core = core_ref[0]
    for left_ref, place in ((own_ref, core), (other_ref, 1 - core)):
        high, low = split(left_ref[...])
        start = pl.multiple_of(place * rows, rows)
        out_ref[pl.ds(start, rows), :] = (
            dot(high, low_ref[...]) + dot(low, high_ref[...]) + dot(high, high_ref[...])
        )


def product(own, other, core, blocks, places, width):
    rows, depth = own.shape
    vmem = pl.BlockSpec(memory_space=pltpu.VMEM)
    return pl.pallas_call(
        functools.partial(product_kernel, places),
        in_specs=[pl.BlockSpec(memory_space=pltpu.SMEM)] + [vmem] * (2 + len(blocks)),
        out_specs=vmem,
        scratch_shapes=[
            pltpu.VMEM((depth, width), jnp.bfloat16),
            pltpu.VMEM((depth, width), jnp.bfloat16),
        ],
        out_shape=jax.ShapeDtypeStruct((2 * rows, width), jnp.float32),
        compiler_params=pltpu.CompilerParams(vmem_limit_bytes=40 * 1024 * 1024),
        cost_estimate=pl.CostEstimate(
            flops=12 * rows * depth * width, bytes_accessed=8 * rows * depth, transcendentals=0
        ),
        name="product",
    )(core, own, other, *blocks)


def body(amplitudes, integrals, pair_list, occupied_energy, virtual_energy):
    rows = amplitudes.shape[0]
    depth, cols = integrals.shape
    core = lax.axis_index("core")
    z = lax.axis_index("z")
    half = cols // 2
    chains = []
    start = 0
    for n, width in enumerate(CHAINS):
        block = lax.dynamic_slice(integrals, (0, core * half + start), (depth, width))
        plus = [block]
        minus = [block]
        ahead = 4 - n % 2
        for _ in range(1, ahead + 1):
            plus.append(shift(plus[-1], "z", -1))
        for _ in range(1, RING - ahead):
            minus.append(shift(minus[-1], "z", 1))
        chains.append(plus + minus[:0:-1])
        start += width
    send = roll_amplitudes(amplitudes, z[None], depth)
    got = lax.all_to_all(send, ("xlo", "y"), split_axis=0, concat_axis=0, tiled=True)
    own = got.reshape(LAYERS * rows, RING * depth)
    other = lax.ppermute(own, "core", [(0, 1), (1, 0)])
    offsets = [s * depth for s in range(RING)]
    sums = []
    for group in GROUPS:
        blocks, places, width = [], [], 0
        for n in group:
            blocks += chains[n]
            places += [(offset, width) for offset in offsets]
            width += CHAINS[n]
        partial = product(own, other, core[None], blocks, tuple(places), width)
        back = lax.all_to_all(
            partial.reshape(2 * LAYERS, rows, width), ("core", "xlo", "y"),
            split_axis=0, concat_axis=0, tiled=True,
        )
        sums.append(jnp.sum(back.reshape(2, LAYERS, rows, width), axis=1))
    ladder = jnp.concatenate([s[c] for c in range(2) for s in sums], axis=1)
    occ_first, occ_second = energy_lookup(pair_list, occupied_energy)
    denominator = virtual_energy[None, :] - occ_first[:, None] - occ_second[:, None]
    return ladder / denominator


def solution(mesh):
    fine = Mesh(mesh.devices.reshape(2, 2, 8, 2, 4), AXES)
    rows = P(AXES, None)
    in_specs = (rows, P(("z", "xlo", "y"), None), rows, P(), P())

    return jax.shard_map(body, mesh=fine, in_specs=in_specs, out_specs=rows, check_vma=False)
```

```python
import functools

import jax
import jax.numpy as jnp
from jax import lax
from jax.experimental import pallas as pl
from jax.experimental.pallas import tpu as pltpu
from jax.sharding import Mesh
from jax.sharding import PartitionSpec as P


AXES = ("xhi", "core", "z", "xlo", "y")
LAYERS = 8
RING = 8
CHAINS = (512, 256, 256)
AHEAD = (4, 3, 3)
STAGES = (
    (((0, 7, None),), ((7, 8, 0), (0, 8, None))),
    (((0, 5, None), (0, 5, None)), ((5, 7, 0), (5, 7, 1)), ((7, 8, 0), (7, 8, 1))),
)
GROUPS = ((0,), (1, 2))
ARRIVAL = (0, 1, 7, 2, 6, 3, 5, 4)
SMEM = pl.BlockSpec(memory_space=pltpu.SMEM)
ANY = pl.BlockSpec(memory_space=pl.ANY)
VMEM_LIMIT = 60 * 1024 * 1024


def energy_lookup(pair_list, occupied_energy):
    occ_index = jnp.arange(occupied_energy.shape[0], dtype=jnp.int32)
    occ_first = jnp.sum(
        jnp.where(pair_list[:, 0:1] == occ_index[None, :], occupied_energy[None, :], 0.0), axis=1
    )
    occ_second = jnp.sum(
        jnp.where(pair_list[:, 1:2] == occ_index[None, :], occupied_energy[None, :], 0.0), axis=1
    )
    return (occ_first, occ_second)


def shift(value, axis, step):
    count = lax.axis_size(axis)
    return lax.ppermute(value, axis, [(i, (i + step) % count) for i in range(count)])


def sort_kernel(z_ref, amp_ref, out_ref, held_ref, in_sem, out_sem):
    depth = out_ref.shape[2] // RING
    span = LAYERS * depth
    loads, stores = [], []
    for p, s in enumerate(ARRIVAL):
        source = pl.multiple_of(lax.rem(z_ref[0] + s, RING) * span, span)
        loads.append(
            pltpu.make_async_copy(
                amp_ref.at[:, pl.ds(source, span)], held_ref.at[:, pl.ds(p * span, span)], in_sem.at[p]
            )
        )
        loads[-1].start()
    for p in range(RING):
        loads[p].wait()
        for layer in range(LAYERS):
            stores.append(
                pltpu.make_async_copy(
                    held_ref.at[:, pl.ds(p * span + layer * depth, depth)],
                    out_ref.at[layer, :, pl.ds(p * depth, depth)],
                    out_sem.at[p * LAYERS + layer],
                )
            )
            stores[-1].start()
    for store in stores:
        store.wait()


def sort_amplitudes(amplitudes, z, depth):
    rows = amplitudes.shape[0]
    return pl.pallas_call(
        sort_kernel,
        in_specs=[SMEM, ANY],
        out_specs=ANY,
        out_shape=jax.ShapeDtypeStruct((LAYERS, rows, RING * depth), jnp.float32),
        scratch_shapes=[
            pltpu.VMEM(amplitudes.shape, jnp.float32),
            pltpu.SemaphoreType.DMA((RING,)),
            pltpu.SemaphoreType.DMA((RING * LAYERS,)),
        ],
        compiler_params=pltpu.CompilerParams(vmem_limit_bytes=VMEM_LIMIT),
        cost_estimate=pl.CostEstimate(flops=0, bytes_accessed=8 * amplitudes.size, transcendentals=0),
        name="sort",
    )(z, amplitudes)


def split(value):
    high = value.astype(jnp.bfloat16)
    low = (value - high.astype(jnp.float32)).astype(jnp.bfloat16)
    return high, low


def product_kernel(jobs, count, final, core_ref, *refs):
    lefts, refs = refs[: len(jobs)], refs[len(jobs) :]
    summed = any(job[2] is not None for job in jobs)
    acc_ref, refs = (refs[0], refs[1:]) if summed else (None, refs)
    blocks, refs = refs[:count], refs[count:]
    out_ref, block_ref, left_ref, sum_ref, high_ref, low_ref, block_sem, left_sem, sum_sem, out_sem = refs
    first = min(job[0] for job in jobs)
    end = max(job[1] for job in jobs)
    span = end - first
    chains = count // span
    depth = block_ref.shape[0] // span
    wide = block_ref.shape[1] // chains
    rows = sum_ref.shape[1]
    middle = first + (span + 1) // 2 if span > 3 else end
    segments = [(first, middle), (middle, end)] if middle < end else [(first, end)]

    def local(lo, hi):
        return slice((lo - first) * depth, (hi - first) * depth)

    block_copies, left_copies, acc_copies = {}, {}, {}
    for n, (lo, hi) in enumerate(segments):
        for p in range(lo, hi):
            for c in range(chains):
                target = block_ref.at[local(p, p + 1), c * wide : (c + 1) * wide]
                block_copies[p, c] = pltpu.make_async_copy(
                    blocks[c * span + p - first], target, block_sem.at[(p - first) * chains + c]
                )
                block_copies[p, c].start()
        for j, job in enumerate(jobs):
            a, b = max(lo, job[0]), min(hi, job[1])
            if a < b:
                left_copies[n, j] = pltpu.make_async_copy(
                    lefts[j].at[:, a * depth : b * depth], left_ref.at[j, :, local(a, b)], left_sem.at[n, j]
                )
                left_copies[n, j].start()
                if job[2] is not None and j not in acc_copies:
                    acc_copies[j] = pltpu.make_async_copy(acc_ref.at[job[2]], sum_ref.at[j], sum_sem.at[j])
                    acc_copies[j].start()
    dot = functools.partial(jnp.dot, preferred_element_type=jnp.float32)
    begun = set()
    copies = []
    for n, (lo, hi) in enumerate(segments):
        for p in range(lo, hi):
            for c in range(chains):
                block_copies[p, c].wait()
        high, low = split(block_ref[local(lo, hi), :])
        high_ref[local(lo, hi), :] = high
        low_ref[local(lo, hi), :] = low
        for j in sorted(range(len(jobs)), key=lambda j: jobs[j][1] - jobs[j][0]):
            a, b = max(lo, jobs[j][0]), min(hi, jobs[j][1])
            if a >= b:
                continue
            left_copies[n, j].wait()
            high, low = split(left_ref[j, :, local(a, b)])
            value = (
                dot(high, low_ref[local(a, b), :])
                + dot(low, high_ref[local(a, b), :])
                + dot(high, high_ref[local(a, b), :])
            )
            if j in begun:
                sum_ref[j] += value
            elif jobs[j][2] is not None:
                acc_copies[j].wait()
                sum_ref[j] += value
            else:
                sum_ref[j] = value
            begun.add(j)
            if b == jobs[j][1]:
                if final:
                    core = core_ref[0]
                    start = pl.multiple_of((core if j == 0 else 1 - core) * rows, rows)
                    target = out_ref.at[pl.ds(start, rows)]
                else:
                    target = out_ref.at[j]
                copies.append(pltpu.make_async_copy(sum_ref.at[j], target, out_sem.at[j]))
                copies[-1].start()
    for copy in copies:
        copy.wait()


def product(core, lefts, jobs, acc, blocks, width, depth, final):
    rows = lefts[0].shape[0]
    span = max(job[1] for job in jobs) - min(job[0] for job in jobs)
    accs = [] if acc is None else [acc]
    shape = (2 * rows, width) if final else (len(jobs), rows, width)
    work = sum(job[1] - job[0] for job in jobs)
    return pl.pallas_call(
        functools.partial(product_kernel, jobs, len(blocks), final),
        in_specs=[SMEM] + [ANY] * (len(lefts) + len(accs) + len(blocks)),
        out_specs=ANY,
        out_shape=jax.ShapeDtypeStruct(shape, jnp.float32),
        scratch_shapes=[
            pltpu.VMEM((span * depth, width), jnp.float32),
            pltpu.VMEM((len(jobs), rows, span * depth), jnp.float32),
            pltpu.VMEM((len(jobs), rows, width), jnp.float32),
            pltpu.VMEM((span * depth, width), jnp.bfloat16),
            pltpu.VMEM((span * depth, width), jnp.bfloat16),
            pltpu.SemaphoreType.DMA((len(blocks),)),
            pltpu.SemaphoreType.DMA((2, len(jobs))),
            pltpu.SemaphoreType.DMA((len(jobs),)),
            pltpu.SemaphoreType.DMA((len(jobs),)),
        ],
        compiler_params=pltpu.CompilerParams(vmem_limit_bytes=VMEM_LIMIT),
        cost_estimate=pl.CostEstimate(
            flops=6 * work * rows * depth * width, bytes_accessed=4 * work * rows * depth, transcendentals=0
        ),
    )(core, *lefts, *accs, *blocks)


def body(amplitudes, integrals, pair_list, occupied_energy, virtual_energy):
    rows = amplitudes.shape[0]
    depth, cols = integrals.shape
    core = lax.axis_index("core")
    z = lax.axis_index("z")
    half = cols // 2
    chains = []
    start = 0
    for n, width in enumerate(CHAINS):
        block = lax.dynamic_slice(integrals, (0, core * half + start), (depth, width))
        plus = [block]
        minus = [block]
        ahead = AHEAD[n]
        for _ in range(1, ahead + 1):
            plus.append(shift(plus[-1], "z", -1))
        for _ in range(1, RING - ahead):
            minus.append(shift(minus[-1], "z", 1))
        ring = plus + minus[:0:-1]
        chains.append([ring[s] for s in ARRIVAL])
        start += width
    send = sort_amplitudes(amplitudes, z[None], depth)
    got = lax.all_to_all(send, ("xlo", "y"), split_axis=0, concat_axis=0, tiled=True)
    own = got.reshape(LAYERS * rows, RING * depth)
    other = lax.ppermute(own, "core", [(0, 1), (1, 0)])
    sums = []
    for g, group in enumerate(GROUPS):
        width = sum(CHAINS[n] for n in group)

        def part(lo, hi):
            return [chains[n][p] for n in group for p in range(lo, hi)]

        acc = None
        for n, jobs in enumerate(STAGES[g]):
            final = n == len(STAGES[g]) - 1
            span = (min(job[0] for job in jobs), max(job[1] for job in jobs))
            acc = product(core[None], [own, other][: len(jobs)], jobs, acc, part(*span), width, depth, final)
        partial = acc
        back = lax.all_to_all(
            partial.reshape(2 * LAYERS, rows, width), ("core", "xlo", "y"),
            split_axis=0, concat_axis=0, tiled=True,
        )
        sums.append(jnp.sum(back.reshape(2, LAYERS, rows, width), axis=1))
    ladder = jnp.concatenate([s[c] for c in range(2) for s in sums], axis=1)
    occ_first, occ_second = energy_lookup(pair_list, occupied_energy)
    denominator = virtual_energy[None, :] - occ_first[:, None] - occ_second[:, None]
    return ladder / denominator


def solution(mesh):
    fine = Mesh(mesh.devices.reshape(2, 2, 8, 2, 4), AXES)
    rows = P(AXES, None)
    in_specs = (rows, P(("z", "xlo", "y"), None), rows, P(), P())

    return jax.shard_map(body, mesh=fine, in_specs=in_specs, out_specs=rows, check_vma=False)
```

```python
import functools

import jax
import jax.numpy as jnp
from jax import lax
from jax.experimental import pallas as pl
from jax.experimental.pallas import tpu as pltpu
from jax.sharding import Mesh
from jax.sharding import PartitionSpec as P


AXES = ("xhi", "core", "z", "xlo", "y")
LAYERS = 8
RING = 8
CHAINS = (512, 256, 256)
AHEAD = (4, 3, 3)
HALVED = ()
STAGES = (
    (((0, 0, 7),), ((1, 0, 7),), ((0, 7, 8), (1, 7, 8))),
    (((0, 0, 5), (1, 0, 5)), ((0, 5, 8), (1, 5, 8))),
)
GROUPS = ((0,), (1, 2))
ARRIVAL = (0, 1, 7, 2, 6, 3, 5, 4)
SMEM = pl.BlockSpec(memory_space=pltpu.SMEM)
ANY = pl.BlockSpec(memory_space=pl.ANY)
VMEM_LIMIT = 60 * 1024 * 1024


def energy_lookup(pair_list, occupied_energy):
    occ_index = jnp.arange(occupied_energy.shape[0], dtype=jnp.int32)
    occ_first = jnp.sum(
        jnp.where(pair_list[:, 0:1] == occ_index[None, :], occupied_energy[None, :], 0.0), axis=1
    )
    occ_second = jnp.sum(
        jnp.where(pair_list[:, 1:2] == occ_index[None, :], occupied_energy[None, :], 0.0), axis=1
    )
    return (occ_first, occ_second)


def shift(value, axis, step):
    count = lax.axis_size(axis)
    return lax.ppermute(value, axis, [(i, (i + step) % count) for i in range(count)])


def sort_kernel(z_ref, amp_ref, out_ref, held_ref, in_sem, out_sem):
    depth = out_ref.shape[2] // RING
    span = LAYERS * depth
    loads, stores = [], []
    for p, s in enumerate(ARRIVAL):
        source = pl.multiple_of(lax.rem(z_ref[0] + s, RING) * span, span)
        loads.append(
            pltpu.make_async_copy(
                amp_ref.at[:, pl.ds(source, span)], held_ref.at[:, pl.ds(p * span, span)], in_sem.at[p]
            )
        )
        loads[-1].start()
    for p in range(RING):
        loads[p].wait()
        for layer in range(LAYERS):
            stores.append(
                pltpu.make_async_copy(
                    held_ref.at[:, pl.ds(p * span + layer * depth, depth)],
                    out_ref.at[layer, :, pl.ds(p * depth, depth)],
                    out_sem.at[p * LAYERS + layer],
                )
            )
            stores[-1].start()
    for store in stores:
        store.wait()


def sort_amplitudes(amplitudes, z, depth):
    rows = amplitudes.shape[0]
    return pl.pallas_call(
        sort_kernel,
        in_specs=[SMEM, ANY],
        out_specs=ANY,
        out_shape=jax.ShapeDtypeStruct((LAYERS, rows, RING * depth), jnp.float32),
        scratch_shapes=[
            pltpu.VMEM(amplitudes.shape, jnp.float32),
            pltpu.SemaphoreType.DMA((RING,)),
            pltpu.SemaphoreType.DMA((RING * LAYERS,)),
        ],
        compiler_params=pltpu.CompilerParams(vmem_limit_bytes=VMEM_LIMIT),
        cost_estimate=pl.CostEstimate(flops=0, bytes_accessed=8 * amplitudes.size, transcendentals=0),
        name="sort",
    )(z, amplitudes)


def split(value):
    high = value.astype(jnp.bfloat16)
    low = (value - high.astype(jnp.float32)).astype(jnp.bfloat16)
    return high, low


def product_kernel(jobs, count, final, core_ref, *refs):
    lefts, refs = refs[: len(jobs)], refs[len(jobs) :]
    summed = [j for j, job in enumerate(jobs) if job[2]]
    accs, refs = dict(zip(summed, refs)), refs[len(summed) :]
    blocks, refs = refs[: sum(count)], refs[sum(count) :]
    outs, refs = (refs[:1], refs[1:]) if final else (refs[: len(jobs)], refs[len(jobs) :])
    block_ref, left_ref, sum_ref, high_ref, low_ref, block_sem, left_sem, sum_sem, out_sem = refs
    first = min(job[0] for job in jobs)
    end = max(job[1] for job in jobs)
    span = end - first
    chains = len(count) // span
    depth = block_ref.shape[0] // span
    wide = block_ref.shape[1] // chains
    rows = sum_ref.shape[1]
    cuts = [first] + [first + cut for cut in (1, 3) if cut < span - 1] + [end]
    segments = list(zip(cuts, cuts[1:]))

    def local(lo, hi):
        return slice((lo - first) * depth, (hi - first) * depth)

    block_copies, left_copies, acc_copies = {}, {}, {}
    for n, (lo, hi) in enumerate(segments):
        for p in range(lo, hi):
            for c in range(chains):
                place = c * span + p - first
                begin = sum(count[:place])
                part = depth // count[place]
                block_copies[p, c] = []
                for k in range(count[place]):
                    row = (p - first) * depth + k * part
                    copy = pltpu.make_async_copy(
                        blocks[begin + k],
                        block_ref.at[row : row + part, c * wide : (c + 1) * wide],
                        block_sem.at[begin + k],
                    )
                    copy.start()
                    block_copies[p, c].append(copy)
        for j, job in enumerate(jobs):
            a, b = max(lo, job[0]), min(hi, job[1])
            if a < b:
                left_copies[n, j] = pltpu.make_async_copy(
                    lefts[j].at[:, a * depth : b * depth], left_ref.at[j, :, local(a, b)], left_sem.at[n, j]
                )
                left_copies[n, j].start()
                if j in accs and j not in acc_copies:
                    acc_copies[j] = pltpu.make_async_copy(accs[j], sum_ref.at[j], sum_sem.at[j])
                    acc_copies[j].start()
    dot = functools.partial(jnp.dot, preferred_element_type=jnp.float32)
    begun = set()
    copies = []
    for n, (lo, hi) in enumerate(segments):
        for p in range(lo, hi):
            for c in range(chains):
                for copy in block_copies[p, c]:
                    copy.wait()
        high, low = split(block_ref[local(lo, hi), :])
        high_ref[local(lo, hi), :] = high
        low_ref[local(lo, hi), :] = low
        for j in sorted(range(len(jobs)), key=lambda j: jobs[j][1] - jobs[j][0]):
            a, b = max(lo, jobs[j][0]), min(hi, jobs[j][1])
            if a >= b:
                continue
            left_copies[n, j].wait()
            high, low = split(left_ref[j, :, local(a, b)])
            value = (
                dot(high, low_ref[local(a, b), :])
                + dot(low, high_ref[local(a, b), :])
                + dot(high, high_ref[local(a, b), :])
            )
            if j in begun:
                sum_ref[j] += value
            elif j in accs:
                acc_copies[j].wait()
                sum_ref[j] += value
            else:
                sum_ref[j] = value
            begun.add(j)
            if b == jobs[j][1]:
                if final:
                    core = core_ref[0]
                    start = pl.multiple_of((core if j == 0 else 1 - core) * rows, rows)
                    target = outs[0].at[pl.ds(start, rows)]
                else:
                    target = outs[j]
                copies.append(pltpu.make_async_copy(sum_ref.at[j], target, out_sem.at[j]))
                copies[-1].start()
    for copy in copies:
        copy.wait()


def product(core, lefts, jobs, accs, blocks, width, depth, final):
    rows = lefts[0].shape[0]
    span = max(job[1] for job in jobs) - min(job[0] for job in jobs)
    shapes = [(2 * rows, width)] if final else [(rows, width)] * len(jobs)
    work = sum(job[1] - job[0] for job in jobs)
    count = tuple(len(b) if isinstance(b, tuple) else 1 for b in blocks)
    blocks = [x for b in blocks for x in (b if isinstance(b, tuple) else (b,))]
    return pl.pallas_call(
        functools.partial(product_kernel, jobs, count, final),
        in_specs=[SMEM] + [ANY] * (len(lefts) + len(accs) + len(blocks)),
        out_specs=[ANY] * len(shapes),
        out_shape=[jax.ShapeDtypeStruct(shape, jnp.float32) for shape in shapes],
        scratch_shapes=[
            pltpu.VMEM((span * depth, width), jnp.float32),
            pltpu.VMEM((len(jobs), rows, span * depth), jnp.float32),
            pltpu.VMEM((len(jobs), rows, width), jnp.float32),
            pltpu.VMEM((span * depth, width), jnp.bfloat16),
            pltpu.VMEM((span * depth, width), jnp.bfloat16),
            pltpu.SemaphoreType.DMA((len(blocks),)),
            pltpu.SemaphoreType.DMA((3, len(jobs))),
            pltpu.SemaphoreType.DMA((len(jobs),)),
            pltpu.SemaphoreType.DMA((len(jobs),)),
        ],
        compiler_params=pltpu.CompilerParams(vmem_limit_bytes=VMEM_LIMIT),
        cost_estimate=pl.CostEstimate(
            flops=6 * work * rows * depth * width, bytes_accessed=4 * work * rows * depth, transcendentals=0
        ),
    )(core, *lefts, *accs, *blocks)


def body(amplitudes, integrals, pair_list, occupied_energy, virtual_energy):
    rows = amplitudes.shape[0]
    depth, cols = integrals.shape
    core = lax.axis_index("core")
    z = lax.axis_index("z")
    half = cols // 2
    chains = []
    start = 0
    for n, width in enumerate(CHAINS):
        block = lax.dynamic_slice(integrals, (0, core * half + start), (depth, width))
        plus = [block]
        minus = [block]
        ahead = AHEAD[n]
        for _ in range(1, ahead + 1):
            plus.append(shift(plus[-1], "z", -1))
        for _ in range(1, min(RING - ahead, 4)):
            minus.append(shift(minus[-1], "z", 1))
        if ahead == 3 and n in HALVED:
            near = plus[3][: depth // 2]
            rest = minus[3][depth // 2 :]
            far = (shift(near, "z", -1), shift(rest, "z", 1))
        elif ahead == 3:
            far = shift(minus[3], "z", 1)
        else:
            far = plus[4]
        ring = plus[:4] + [far] + minus[:0:-1]
        chains.append([ring[s] for s in ARRIVAL])
        start += width
    send = sort_amplitudes(amplitudes, z[None], depth)
    got = lax.all_to_all(send, ("xlo", "y"), split_axis=0, concat_axis=0, tiled=True)
    own = got.reshape(LAYERS * rows, RING * depth)
    other = lax.ppermute(own, "core", [(0, 1), (1, 0)])
    sums = []
    for g, group in enumerate(GROUPS):
        width = sum(CHAINS[n] for n in group)

        def part(lo, hi):
            return [chains[n][p] for n in group for p in range(lo, hi)]

        lefts = (own, other)
        accs = [None, None]
        for n, stage in enumerate(STAGES[g]):
            final = n == len(STAGES[g]) - 1
            span = (min(job[1] for job in stage), max(job[2] for job in stage))
            jobs = tuple((lo, hi, accs[k] is not None) for k, lo, hi in stage)
            given = [accs[k] for k, _, _ in stage if accs[k] is not None]
            results = product(
                core[None], [lefts[k] for k, _, _ in stage], jobs, given, part(*span), width, depth,
                final,
            )
            if final:
                partial = results[0]
            else:
                for (k, _, _), result in zip(stage, results):
                    accs[k] = result
        back = lax.all_to_all(
            partial.reshape(2 * LAYERS, rows, width), ("core", "xlo", "y"),
            split_axis=0, concat_axis=0, tiled=True,
        )
        sums.append(jnp.sum(back.reshape(2, LAYERS, rows, width), axis=1))
    ladder = jnp.concatenate([s[c] for c in range(2) for s in sums], axis=1)
    occ_first, occ_second = energy_lookup(pair_list, occupied_energy)
    denominator = virtual_energy[None, :] - occ_first[:, None] - occ_second[:, None]
    return ladder / denominator


def solution(mesh):
    fine = Mesh(mesh.devices.reshape(2, 2, 8, 2, 4), AXES)
    rows = P(AXES, None)
    in_specs = (rows, P(("z", "xlo", "y"), None), rows, P(), P())

    return jax.shard_map(body, mesh=fine, in_specs=in_specs, out_specs=rows, check_vma=False)
```

```python
import functools

import jax
import jax.numpy as jnp
from jax import lax
from jax.experimental import pallas as pl
from jax.experimental.pallas import tpu as pltpu
from jax.sharding import Mesh
from jax.sharding import PartitionSpec as P


AXES = ("xhi", "core", "z", "xlo", "y")
LAYERS = 8
RING = 8
CHAINS = (512, 256, 256)
AHEAD = (4, 3, 3)
HALVED = ()
STAGES = (
    (((0, 0, 7),), ((1, 0, 7),), ((0, 7, 8), (1, 7, 8))),
    (((0, 0, 5), (1, 0, 5)), ((0, 5, 8), (1, 5, 8))),
)
GROUPS = ((0,), (1, 2))
ARRIVAL = (0, 1, 7, 2, 6, 3, 5, 4)
VMEM = pl.BlockSpec(memory_space=pltpu.VMEM)
SMEM = pl.BlockSpec(memory_space=pltpu.SMEM)
ANY = pl.BlockSpec(memory_space=pl.ANY)
CUTS = (1, 3, 5)
RESIDENT = ()
SMALL = (0, 1)
SMALL_LIMIT = 16 * 1024 * 1024
VMEM_LIMIT = 60 * 1024 * 1024


def energy_lookup(pair_list, occupied_energy):
    occ_index = jnp.arange(occupied_energy.shape[0], dtype=jnp.int32)
    occ_first = jnp.sum(
        jnp.where(pair_list[:, 0:1] == occ_index[None, :], occupied_energy[None, :], 0.0), axis=1
    )
    occ_second = jnp.sum(
        jnp.where(pair_list[:, 1:2] == occ_index[None, :], occupied_energy[None, :], 0.0), axis=1
    )
    return (occ_first, occ_second)


def shift(value, axis, step):
    count = lax.axis_size(axis)
    return lax.ppermute(value, axis, [(i, (i + step) % count) for i in range(count)])


def sort_kernel(z_ref, amp_ref, out_ref, held_ref, in_sem, out_sem):
    depth = out_ref.shape[2] // RING
    span = LAYERS * depth
    loads, stores = [], []
    for p, s in enumerate(ARRIVAL):
        source = pl.multiple_of(lax.rem(z_ref[0] + s, RING) * span, span)
        loads.append(
            pltpu.make_async_copy(
                amp_ref.at[:, pl.ds(source, span)], held_ref.at[:, pl.ds(p * span, span)], in_sem.at[p]
            )
        )
        loads[-1].start()
    for p in range(RING):
        loads[p].wait()
        for layer in range(LAYERS):
            stores.append(
                pltpu.make_async_copy(
                    held_ref.at[:, pl.ds(p * span + layer * depth, depth)],
                    out_ref.at[layer, :, pl.ds(p * depth, depth)],
                    out_sem.at[p * LAYERS + layer],
                )
            )
            stores[-1].start()
    for store in stores:
        store.wait()


def sort_amplitudes(amplitudes, z, depth):
    rows = amplitudes.shape[0]
    return pl.pallas_call(
        sort_kernel,
        in_specs=[SMEM, ANY],
        out_specs=ANY,
        out_shape=jax.ShapeDtypeStruct((LAYERS, rows, RING * depth), jnp.float32),
        scratch_shapes=[
            pltpu.VMEM(amplitudes.shape, jnp.float32),
            pltpu.SemaphoreType.DMA((RING,)),
            pltpu.SemaphoreType.DMA((RING * LAYERS,)),
        ],
        compiler_params=pltpu.CompilerParams(vmem_limit_bytes=VMEM_LIMIT),
        cost_estimate=pl.CostEstimate(flops=0, bytes_accessed=8 * amplitudes.size, transcendentals=0),
        name="sort",
    )(z, amplitudes)


def split(value):
    high = value.astype(jnp.bfloat16)
    low = (value - high.astype(jnp.float32)).astype(jnp.bfloat16)
    return high, low


def product_kernel(jobs, count, final, resident, core_ref, *refs):
    lefts, refs = refs[: len(jobs)], refs[len(jobs) :]
    summed = [j for j, job in enumerate(jobs) if job[2]]
    accs, refs = dict(zip(summed, refs)), refs[len(summed) :]
    blocks, refs = refs[: sum(count)], refs[sum(count) :]
    outs, refs = (refs[:1], refs[1:]) if final else (refs[: len(jobs)], refs[len(jobs) :])
    left_ref, sum_ref, high_ref, low_ref, left_high_ref, left_low_ref = refs[:6]
    block_ref, block_sem, left_sem, sum_sem, out_sem = refs[6:]
    first = min(job[0] for job in jobs)
    end = max(job[1] for job in jobs)
    span = end - first
    chains = len(count) // span
    depth = high_ref.shape[0] // span
    wide = high_ref.shape[1] // chains
    rows = sum_ref.shape[1]
    cuts = [first] + [first + cut for cut in CUTS if cut < span - 1] + [end]
    segments = list(zip(cuts, cuts[1:]))

    def local(lo, hi):
        return slice((lo - first) * depth, (hi - first) * depth)

    block_copies, left_copies, acc_copies = {}, {}, {}
    for n, (lo, hi) in enumerate(segments):
        for p in range(lo, hi):
            for c in range(chains):
                place = c * span + p - first
                begin = sum(count[:place])
                part = depth // count[place]
                block_copies[p, c] = []
                for k in range(0 if resident else count[place]):
                    row = (p - first) * depth + k * part
                    copy = pltpu.make_async_copy(
                        blocks[begin + k],
                        block_ref.at[row : row + part, c * wide : (c + 1) * wide],
                        block_sem.at[begin + k],
                    )
                    copy.start()
                    block_copies[p, c].append(copy)
        for j, job in enumerate(jobs):
            a, b = max(lo, job[0]), min(hi, job[1])
            if a < b:
                left_copies[n, j] = pltpu.make_async_copy(
                    lefts[j].at[:, a * depth : b * depth], left_ref.at[j, :, local(a, b)], left_sem.at[n, j]
                )
                left_copies[n, j].start()
                if j in accs and j not in acc_copies:
                    acc_copies[j] = pltpu.make_async_copy(accs[j], sum_ref.at[j], sum_sem.at[j])
                    acc_copies[j].start()
    dot = functools.partial(jnp.dot, preferred_element_type=jnp.float32)
    begun = set()
    copies = []

    def prepare(n):
        lo, hi = segments[n]
        for p in range(lo, hi):
            for c in range(chains):
                for copy in block_copies[p, c]:
                    copy.wait()
        for j in range(len(jobs)):
            if (n, j) in left_copies:
                left_copies[n, j].wait()

    def pieces(n):
        lo, hi = segments[n]
        if resident:
            for p in range(lo, hi):
                row = local(p, p + 1)
                high_ref[row, :], low_ref[row, :] = split(blocks[p - first][...])
        else:
            high_ref[local(lo, hi), :], low_ref[local(lo, hi), :] = split(block_ref[local(lo, hi), :])
        for j, job in enumerate(jobs):
            if (n, j) in left_copies:
                part = local(max(lo, job[0]), min(hi, job[1]))
                left_high_ref[j, :, part], left_low_ref[j, :, part] = split(left_ref[j, :, part])

    def multiply(n, j):
        part = local(max(segments[n][0], jobs[j][0]), min(segments[n][1], jobs[j][1]))
        return (
            dot(left_high_ref[j, :, part], low_ref[part, :])
            + dot(left_low_ref[j, :, part], high_ref[part, :])
            + dot(left_high_ref[j, :, part], high_ref[part, :])
        )

    prepare(0)
    for j in acc_copies:
        acc_copies[j].wait()
    pieces(0)
    for n, (lo, hi) in enumerate(segments):
        if n + 1 < len(segments):
            prepare(n + 1)
            pieces(n + 1)
        for j in range(len(jobs)):
            if (n, j) not in left_copies:
                continue
            if j in begun or j in accs:
                sum_ref[j] += multiply(n, j)
            else:
                sum_ref[j] = multiply(n, j)
            begun.add(j)
            if min(hi, jobs[j][1]) == jobs[j][1]:
                if final:
                    core = core_ref[0]
                    start = pl.multiple_of((core if j == 0 else 1 - core) * rows, rows)
                    target = outs[0].at[pl.ds(start, rows)]
                else:
                    target = outs[j]
                copies.append(pltpu.make_async_copy(sum_ref.at[j], target, out_sem.at[j]))
                copies[-1].start()
    for copy in copies:
        copy.wait()


def product(core, lefts, jobs, accs, blocks, width, depth, final, resident, small):
    rows = lefts[0].shape[0]
    span = max(job[1] for job in jobs) - min(job[0] for job in jobs)
    shapes = [(2 * rows, width)] if final else [(rows, width)] * len(jobs)
    work = sum(job[1] - job[0] for job in jobs)
    count = tuple(len(b) if isinstance(b, tuple) else 1 for b in blocks)
    blocks = [x for b in blocks for x in (b if isinstance(b, tuple) else (b,))]
    return pl.pallas_call(
        functools.partial(product_kernel, jobs, count, final, resident),
        in_specs=[SMEM] + [ANY] * (len(lefts) + len(accs)) + [VMEM if resident else ANY] * len(blocks),
        out_specs=[ANY] * len(shapes),
        out_shape=[jax.ShapeDtypeStruct(shape, jnp.float32) for shape in shapes],
        scratch_shapes=[
            pltpu.VMEM((len(jobs), rows, span * depth), jnp.float32),
            pltpu.VMEM((len(jobs), rows, width), jnp.float32),
            pltpu.VMEM((span * depth, width), jnp.bfloat16),
            pltpu.VMEM((span * depth, width), jnp.bfloat16),
            pltpu.VMEM((len(jobs), rows, span * depth), jnp.bfloat16),
            pltpu.VMEM((len(jobs), rows, span * depth), jnp.bfloat16),
            pltpu.VMEM((8, 128) if resident else (span * depth, width), jnp.float32),
            pltpu.SemaphoreType.DMA((len(blocks),)),
            pltpu.SemaphoreType.DMA((len(CUTS) + 1, len(jobs))),
            pltpu.SemaphoreType.DMA((len(jobs),)),
            pltpu.SemaphoreType.DMA((len(jobs),)),
        ],
        compiler_params=pltpu.CompilerParams(vmem_limit_bytes=SMALL_LIMIT if small else VMEM_LIMIT),
        cost_estimate=pl.CostEstimate(
            flops=6 * work * rows * depth * width, bytes_accessed=4 * work * rows * depth, transcendentals=0
        ),
    )(core, *lefts, *accs, *blocks)


def body(amplitudes, integrals, pair_list, occupied_energy, virtual_energy):
    rows = amplitudes.shape[0]
    depth, cols = integrals.shape
    core = lax.axis_index("core")
    z = lax.axis_index("z")
    half = cols // 2
    chains = []
    start = 0
    for n, width in enumerate(CHAINS):
        block = lax.dynamic_slice(integrals, (0, core * half + start), (depth, width))
        plus = [block]
        minus = [block]
        ahead = AHEAD[n]
        for _ in range(1, ahead + 1):
            plus.append(shift(plus[-1], "z", -1))
        for _ in range(1, min(RING - ahead, 4)):
            minus.append(shift(minus[-1], "z", 1))
        if ahead == 3 and n in HALVED:
            near = plus[3][: depth // 2]
            rest = minus[3][depth // 2 :]
            far = (shift(near, "z", -1), shift(rest, "z", 1))
        elif ahead == 3:
            far = shift(minus[3], "z", 1)
        else:
            far = plus[4]
        ring = plus[:4] + [far] + minus[:0:-1]
        chains.append([ring[s] for s in ARRIVAL])
        start += width
    send = sort_amplitudes(amplitudes, z[None], depth)
    got = lax.all_to_all(send, ("xlo", "y"), split_axis=0, concat_axis=0, tiled=True)
    own = got.reshape(LAYERS * rows, RING * depth)
    other = lax.ppermute(own, "core", [(0, 1), (1, 0)])
    sums = []
    for g, group in enumerate(GROUPS):
        width = sum(CHAINS[n] for n in group)

        def part(lo, hi):
            return [chains[n][p] for n in group for p in range(lo, hi)]

        lefts = (own, other)
        accs = [None, None]
        for n, stage in enumerate(STAGES[g]):
            final = n == len(STAGES[g]) - 1
            span = (min(job[1] for job in stage), max(job[2] for job in stage))
            jobs = tuple((lo, hi, accs[k] is not None) for k, lo, hi in stage)
            given = [accs[k] for k, _, _ in stage if accs[k] is not None]
            results = product(
                core[None], [lefts[k] for k, _, _ in stage], jobs, given, part(*span), width, depth,
                final, g in RESIDENT, g in SMALL,
            )
            if final:
                partial = results[0]
            else:
                for (k, _, _), result in zip(stage, results):
                    accs[k] = result
        back = lax.all_to_all(
            partial.reshape(2 * LAYERS, rows, width), ("core", "xlo", "y"),
            split_axis=0, concat_axis=0, tiled=True,
        )
        sums.append(jnp.sum(back.reshape(2, LAYERS, rows, width), axis=1))
    ladder = jnp.concatenate([s[c] for c in range(2) for s in sums], axis=1)
    occ_first, occ_second = energy_lookup(pair_list, occupied_energy)
    denominator = virtual_energy[None, :] - occ_first[:, None] - occ_second[:, None]
    return ladder / denominator


def solution(mesh):
    fine = Mesh(mesh.devices.reshape(2, 2, 8, 2, 4), AXES)
    rows = P(AXES, None)
    in_specs = (rows, P(("z", "xlo", "y"), None), rows, P(), P())

    return jax.shard_map(body, mesh=fine, in_specs=in_specs, out_specs=rows, check_vma=False)
```
